128 devices in a mesh: box: 32 (over z_hi, y, x), dir: 4 (over z_lo, core).
Axes of the slice: x: 4, y: 4, z: 4 (z_hi: 2, z_lo: 2; z = z_hi * 2 + z_lo), core: 2. Of those that a mesh axis runs over, the one named last changes fastest.
Arguments:
- low_field: float32 [8192, 2, 64, 128], P('box', None, 'dir'), may hold values from -6 to 6
- far_src_low: int32 [8192, 8], P('box'), may hold values from -1 to 8191, as said below
- far_class_low: int32 [8192, 8], P('box'), may hold values from 0 to 15
- table_low: float32 [16, 2, 64, 128], P(None, None, 'dir'), may hold values from -3 to 3
- far_src_mid: int32 [1024, 8], P('box'), may hold values from -1 to 1023, as said below
- far_class_mid: int32 [1024, 8], P('box'), may hold values from 0 to 15
- table_mid: float32 [16, 2, 128, 256], P(None, None, 'dir'), may hold values from -3 to 3
- far_src_top: int32 [128, 8], P('box'), may hold values from -1 to 127, as said below
- far_class_top: int32 [128, 8], P('box'), may hold values from 0 to 15
- table_top: float32 [16, 2, 256, 512], P(None, None, 'dir'), may hold values from -3 to 3
Outputs:
- incoming_low: float32 [8192, 2, 64, 128], P('box', None, 'dir')
- incoming_mid: float32 [1024, 2, 128, 256], P('box', None, 'dir')
- incoming_top: float32 [128, 2, 256, 512], P('box', None, 'dir')
The draws below stay inside these ranges and needn't reach their ends.
Inputs may be any that keep to these rules, and one draw needn't show every extreme that they name: `far_src_low`: each box has 8 slots; -1 marks an empty slot and empty slots follow the occupied ones; every box has one occupied slot or more; an occupied slot names a box of the same block of 256 consecutive boxes or of a block beside it; in every draw some box fills all slots. `far_src_mid`: as for the finest level, with blocks of 32 consecutive boxes. `far_src_top`: as for the finest level, with blocks of 4 consecutive boxes.
All inputs are finite; a program needn't handle non-finite values.
Results may differ from the reference program's by a relative error of at most 0.0003.
Values sent between devices are 32-bit elements; how exact they have to be, the bound alone decides.
No kernel may reach another device: no remote copies, remote signals or barrier semaphores. Data moves between devices by JAX's collectives and lax.ppermute only.
A program may use at most 128 MiB of HBM per device.

```python
import jax
import jax.numpy as jnp
from jax import lax

THETA_LOW = 64
PHI_LOW = 128
THETA_MID = 128
PHI_MID = 256
THETA_TOP = 256
PHI_TOP = 512
TOP_DEV = 4
MID_DEV = 32
LOW_DEV = 256
TOP_BOXES = 128
MID_BOXES = 1024
LOW_BOXES = 8192
LIST_SLOTS = 8
CLASSES = 16
N_BOX = 32


def far_lists(key, boxes_total, block_size):
    blocks = boxes_total // block_size
    subkeys = jax.random.split(key, 6)
    capacity = jax.random.randint(subkeys[0], (blocks,), 2, LIST_SLOTS + 1)
    busiest = jax.random.randint(subkeys[1], (), 0, blocks)
    capacity = jnp.where(jnp.arange(blocks, dtype=jnp.int32) == busiest, LIST_SLOTS, capacity)
    owners = jnp.arange(boxes_total, dtype=jnp.int32) // block_size
    box_capacity = capacity[owners]
    draws = jax.random.randint(subkeys[2], (boxes_total,), 0, 1 << 20)
    counts = 1 + draws % box_capacity
    counts = jnp.where(jnp.arange(boxes_total, dtype=jnp.int32) == busiest * block_size, LIST_SLOTS, counts)
    offsets = jax.random.randint(subkeys[3], (boxes_total, LIST_SLOTS), -1, 2)
    target = jnp.clip(owners[:, None] + offsets, 0, blocks - 1)
    within = jax.random.randint(subkeys[4], (boxes_total, LIST_SLOTS), 0, block_size)
    sources = target * block_size + within
    occupied = jnp.arange(LIST_SLOTS, dtype=jnp.int32)[None, :] < counts[:, None]
    sources = jnp.where(occupied, sources, -1).astype(jnp.int32)
    classes = jax.random.randint(subkeys[5], (boxes_total, LIST_SLOTS), 0, CLASSES).astype(jnp.int32)
    return (sources, classes)


def draw_far_src_low(key, part):
    return far_lists(jax.random.fold_in(key, 101), LOW_BOXES, LOW_DEV)[0]


def draw_far_class_low(key, part):
    return far_lists(jax.random.fold_in(key, 101), LOW_BOXES, LOW_DEV)[1]


def draw_far_src_mid(key, part):
    return far_lists(jax.random.fold_in(key, 202), MID_BOXES, MID_DEV)[0]


def draw_far_class_mid(key, part):
    return far_lists(jax.random.fold_in(key, 202), MID_BOXES, MID_DEV)[1]


def draw_far_src_top(key, part):
    return far_lists(jax.random.fold_in(key, 303), TOP_BOXES, TOP_DEV)[0]


def draw_far_class_top(key, part):
    return far_lists(jax.random.fold_in(key, 303), TOP_BOXES, TOP_DEV)[1]


def steps_of(stream_key, extent, shards, low, top_value):
    loudness = 1.0
    for dim, parts in shards:
        heights = jax.random.uniform(jax.random.fold_in(jax.random.fold_in(stream_key, 6), dim), (parts,), jnp.float32, low / len(shards), top_value / len(shards))
        loudness = loudness * jnp.repeat(jnp.exp(heights), extent[dim] // parts).reshape((-1,) + (1,) * (len(extent) - 1 - dim))
    return loudness


def scatter_about(own_key, shape, width, bound, pieces=(), held_as=jnp.bfloat16):
    array = jax.random.normal(own_key, shape, jnp.float32) * width
    if len(pieces) > 0:
        array = steps_of(own_key, shape, pieces, -0.22, 0.18) * array
    return jnp.clip(array, min=-bound, max=bound).astype(held_as)


def setup_inputs(seed: int = 0) -> dict:
    keys = jax.random.split(jax.random.key(seed), 11)
    return {
        "low_field": scatter_about(keys[0], (LOW_BOXES, 2, THETA_LOW, PHI_LOW), 1.0, 6.0, ((0, 32), (2, 4)), jnp.float32),
        "far_src_low": draw_far_src_low(jax.random.fold_in(keys[10], 71), 0),
        "far_class_low": draw_far_class_low(jax.random.fold_in(keys[10], 71), 0),
        "table_low": scatter_about(keys[3], (CLASSES, 2, THETA_LOW, PHI_LOW), 0.5, 3.0, ((2, 4),), jnp.float32),
        "far_src_mid": draw_far_src_mid(jax.random.fold_in(keys[10], 71), 0),
        "far_class_mid": draw_far_class_mid(jax.random.fold_in(keys[10], 71), 0),
        "table_mid": scatter_about(keys[6], (CLASSES, 2, THETA_MID, PHI_MID), 0.5, 3.0, ((2, 4),), jnp.float32),
        "far_src_top": draw_far_src_top(jax.random.fold_in(keys[10], 71), 0),
        "far_class_top": draw_far_class_top(jax.random.fold_in(keys[10], 71), 0),
        "table_top": scatter_about(keys[9], (CLASSES, 2, THETA_TOP, PHI_TOP), 0.5, 3.0, ((2, 4),), jnp.float32),
    }


def interp_matrix(samples):
    fine_index = jnp.arange(2 * samples, dtype=jnp.int32)[:, None]
    coarse_index = jnp.arange(samples, dtype=jnp.int32)[None, :]
    offsets = fine_index - 2 * coarse_index
    numerator = jnp.where(offsets % 2 == 0, 0.0, jnp.where(offsets % 4 == 1, 1.0, -1.0)).astype(jnp.float32)
    half_angle = jnp.pi * offsets.astype(jnp.float32) / (2.0 * samples)
    safe_angle = jnp.where(offsets == 0, 1.0, half_angle)
    values = numerator * jnp.cos(safe_angle) / (samples * jnp.sin(safe_angle))
    return jnp.where(offsets == 0, 1.0, values).astype(jnp.float32)


def shift_factors(polar_rows, polar_count, azimuth_count):
    polar = jnp.pi * (polar_rows.astype(jnp.float32) + 0.5) / polar_count
    azimuth = 2.0 * jnp.pi * jnp.arange(azimuth_count, dtype=jnp.int32).astype(jnp.float32) / azimuth_count
    octant = jnp.arange(8, dtype=jnp.int32)
    sign_x = ((octant % 2) * 2 - 1).astype(jnp.float32)[:, None, None]
    sign_y = (((octant // 2) % 2) * 2 - 1).astype(jnp.float32)[:, None, None]
    sign_z = (((octant // 4) % 2) * 2 - 1).astype(jnp.float32)[:, None, None]
    wavenumber = polar_count / 8.0
    sin_polar = jnp.sin(polar)[None, :, None]
    cos_polar = jnp.cos(polar)[None, :, None]
    phases = wavenumber * (sign_x * sin_polar * jnp.cos(azimuth)[None, None, :] + sign_y * sin_polar * jnp.sin(azimuth)[None, None, :] + sign_z * cos_polar)
    return jnp.cos(phases), jnp.sin(phases)


def combine(refined, cosines, sine_part):
    groups = refined.reshape((refined.shape[0] // 8, 8) + refined.shape[1:])
    real_part = jnp.sum(cosines * groups[:, :, 0] - sine_part * groups[:, :, 1], axis=1)
    imag_part = jnp.sum(cosines * groups[:, :, 1] + sine_part * groups[:, :, 0], axis=1)
    return jnp.stack([real_part, imag_part], axis=1)


def slot_term(sources_rows, factor, occupied_col):
    real_part = factor[:, 0] * sources_rows[:, 0] - factor[:, 1] * sources_rows[:, 1]
    imag_part = factor[:, 0] * sources_rows[:, 1] + factor[:, 1] * sources_rows[:, 0]
    stacked = jnp.stack([real_part, imag_part], axis=1)
    return jnp.where(occupied_col[:, None, None, None], stacked, 0.0)


def aggregate_reference(children):
    polar_count = children.shape[2]
    azimuth_count = children.shape[3]
    polar_matrix = interp_matrix(polar_count)
    azimuth_matrix = interp_matrix(azimuth_count)
    cosines, sine_part = shift_factors(jnp.arange(2 * polar_count, dtype=jnp.int32), 2 * polar_count, 2 * azimuth_count)

    def one_block(members):
        half_done = jnp.einsum("ak,bckp->bcap", polar_matrix, members, precision=lax.Precision.HIGHEST)
        refined = jnp.einsum("bcap,qp->bcaq", half_done, azimuth_matrix, precision=lax.Precision.HIGHEST)
        return combine(refined, cosines, sine_part)

    block_size = children.shape[0] // N_BOX
    grouped = children.reshape((N_BOX, block_size) + children.shape[1:])
    parents = lax.map(one_block, grouped)
    return parents.reshape((children.shape[0] // 8,) + parents.shape[2:])


def translate_reference(pattern, far_src, far_class, operator_table):
    block_size = pattern.shape[0] // N_BOX

    def one_block(lists):
        sources, classes = lists
        occupied = sources >= 0
        position = jnp.where(occupied, sources, 0).astype(jnp.int32)
        summed = jnp.zeros((block_size,) + pattern.shape[1:], jnp.float32)
        for slot_index in range(sources.shape[1]):
            sources_rows = jnp.take(pattern, position[:, slot_index], axis=0)
            factor = jnp.take(operator_table, classes[:, slot_index], axis=0)
            summed = summed + slot_term(sources_rows, factor, occupied[:, slot_index])
        return summed

    lists = (far_src.reshape(N_BOX, block_size, -1), far_class.reshape(N_BOX, block_size, -1))
    result = lax.map(one_block, lists)
    return result.reshape(pattern.shape)


def reference(low_field, far_src_low, far_class_low, table_low, far_src_mid, far_class_mid, table_mid, far_src_top, far_class_top, table_top):
    incoming_low = translate_reference(low_field, far_src_low, far_class_low, table_low)
    mid_field = aggregate_reference(low_field)
    incoming_mid = translate_reference(mid_field, far_src_mid, far_class_mid, table_mid)
    top_field = aggregate_reference(mid_field)
    incoming_top = translate_reference(top_field, far_src_top, far_class_top, table_top)
    return (incoming_low, incoming_mid, incoming_top)
```

```python
import jax
import jax.numpy as jnp
from jax import lax
from jax.experimental import pallas as pl
from jax.experimental.pallas import tpu as pltpu
from jax.sharding import PartitionSpec as P

SLOTS = 8


def interp_matrix(samples):
    fine_index = jnp.arange(2 * samples, dtype=jnp.int32)[:, None]
    coarse_index = jnp.arange(samples, dtype=jnp.int32)[None, :]
    offsets = fine_index - 2 * coarse_index
    numerator = jnp.where(offsets % 2 == 0, 0.0, jnp.where(offsets % 4 == 1, 1.0, -1.0)).astype(
        jnp.float32
    )
    half_angle = jnp.pi * offsets.astype(jnp.float32) / (2.0 * samples)
    safe_angle = jnp.where(offsets == 0, 1.0, half_angle)
    values = numerator * jnp.cos(safe_angle) / (samples * jnp.sin(safe_angle))
    return jnp.where(offsets == 0, 1.0, values)


def shift_factors(polar_rows, polar_count, azimuth_count):
    polar = jnp.pi * (polar_rows.astype(jnp.float32) + 0.5) / polar_count
    azimuth = (
        2.0
        * jnp.pi
        * jnp.arange(azimuth_count, dtype=jnp.int32).astype(jnp.float32)
        / azimuth_count
    )
    octant = jnp.arange(8, dtype=jnp.int32)
    sign_x = (octant % 2 * 2 - 1).astype(jnp.float32)[:, None, None]
    sign_y = (octant // 2 % 2 * 2 - 1).astype(jnp.float32)[:, None, None]
    sign_z = (octant // 4 % 2 * 2 - 1).astype(jnp.float32)[:, None, None]
    wavenumber = polar_count / 8.0
    sin_polar = jnp.sin(polar)[None, :, None]
    cos_polar = jnp.cos(polar)[None, :, None]
    phases = wavenumber * (
        sign_x * sin_polar * jnp.cos(azimuth)[None, None, :]
        + sign_y * sin_polar * jnp.sin(azimuth)[None, None, :]
        + sign_z * cos_polar
    )
    return (jnp.cos(phases), jnp.sin(phases))


def combine(refined, cosines, sine_part):
    groups = refined.reshape((refined.shape[0] // 8, 8) + refined.shape[1:])
    real_part = jnp.sum(cosines * groups[:, :, 0] - sine_part * groups[:, :, 1], axis=1)
    imag_part = jnp.sum(cosines * groups[:, :, 1] + sine_part * groups[:, :, 0], axis=1)
    return jnp.stack([real_part, imag_part], axis=1)


def aggregate(gathered):
    polar_count, azimuth_count = gathered.shape[2:]
    polar_matrix = interp_matrix(polar_count)
    azimuth_matrix = interp_matrix(azimuth_count)
    half_done = jnp.einsum("ak,bckp->bcap", polar_matrix, gathered, precision=lax.Precision.HIGHEST)
    refined = jnp.einsum(
        "bcap,qp->bcaq", half_done, azimuth_matrix, precision=lax.Precision.HIGHEST
    )
    cosines, sine_part = shift_factors(
        jnp.arange(2 * polar_count, dtype=jnp.int32), 2 * polar_count, 2 * azimuth_count
    )
    return combine(refined, cosines, sine_part)


def to_boxes(pattern):
    return lax.all_to_all(pattern, "dir", split_axis=0, concat_axis=2, tiled=True)


def to_polar(pattern):
    return lax.all_to_all(pattern, "dir", split_axis=2, concat_axis=0, tiled=True)


def neighbour_pairs(step, flip):
    boxes, dirs = lax.axis_size("box"), lax.axis_size("dir")
    half = boxes // 2
    pairs = []
    for i in range(boxes):
        j = i + step
        if 0 <= j < boxes:
            crossing = {i, j} == {half - 1, half}
            for d in range(dirs):
                pairs.append((i * dirs + d, j * dirs + (d ^ flip if crossing else d)))
    return pairs


def fix_pairs(box, flip):
    dirs = lax.axis_size("dir")
    return [(box * dirs + d, box * dirs + (d ^ flip)) for d in range(dirs)]


def halo(pattern, flip):
    axes = ("box", "dir")
    before = lax.ppermute(pattern, axes, neighbour_pairs(1, flip))
    after = lax.ppermute(pattern, axes, neighbour_pairs(-1, flip))
    if not flip:
        return (before,), (after,)
    half = lax.axis_size("box") // 2
    before_fixed = lax.ppermute(before, axes, fix_pairs(half, flip))
    after_fixed = lax.ppermute(after, axes, fix_pairs(half - 1, flip))
    return (before, before_fixed), (after, after_fixed)


def translate_kernel(block, n_groups, chunks, step_boxes, *refs):
    flags_ref, index_ref, class_ref = refs[:3]
    own_ref, table_ref = refs[3:5]
    per = 2 if len(refs) > 5 + 2 * n_groups + 4 else 1
    before_refs = refs[5 : 5 + n_groups * per]
    after_refs = refs[5 + n_groups * per : 5 + 2 * n_groups * per]
    out_ref, extended, table, sem = refs[5 + 2 * n_groups * per :]
    step = pl.program_id(0)
    size = block // n_groups

    def arrays(kind):
        copies = [
            (own_ref, extended.at[pl.ds(block, block)], sem.at[0]),
            (table_ref, table, sem.at[1]),
        ]
        for g in range(n_groups):
            for side, side_refs in enumerate((before_refs, after_refs)):
                ref = side_refs[g * per + (kind[side] if per == 2 else 0)]
                start = (0 if side == 0 else 2 * block) + g * size
                copies.append((ref, extended.at[pl.ds(start, size)], sem.at[2 + 2 * g + side]))
        return copies

    @pl.when(step == 0)
    def _():
        extended[3 * block] = jnp.zeros(extended.shape[1:], jnp.float32)
        shared = arrays((0, 0))
        for src, dst, s in shared[:2]:
            pltpu.make_async_copy(src, dst, s).start()
        for side in range(2):
            if per == 1:
                for src, dst, s in shared[2 + side :: 2]:
                    pltpu.make_async_copy(src, dst, s).start()
            else:
                for kind in range(2):

                    @pl.when(flags_ref[side] == kind)
                    def _(side=side, kind=kind):
                        for src, dst, s in arrays((kind, kind))[2 + side :: 2]:
                            pltpu.make_async_copy(src, dst, s).start()

        for src, dst, s in shared:
            pltpu.make_async_copy(src, dst, s).wait()

    rows, lanes = chunks
    all_rows, all_lanes = extended.shape[2:]

    def one_box(b, carry):
        first = (step * step_boxes + b) * SLOTS
        indices = [index_ref[first + m] for m in range(SLOTS)]
        classes = [class_ref[first + m] for m in range(SLOTS)]

        def one_chunk(c, carry):
            r = pl.ds(pl.multiple_of(c * rows, 8), rows)
            real = imag = None
            for i, k in zip(indices, classes):
                p_re, p_im = extended[i, 0, r, :], extended[i, 1, r, :]
                q_re, q_im = table[k, 0, r, :], table[k, 1, r, :]
                re = q_re * p_re - q_im * p_im
                im = q_re * p_im + q_im * p_re
                real = re if real is None else real + re
                imag = im if imag is None else imag + im
            out_ref[b, 0, r, :] = real
            out_ref[b, 1, r, :] = imag
            return carry

        if all_rows == rows:
            return one_chunk(0, carry)
        return lax.fori_loop(0, all_rows // rows, one_chunk, carry)

    lax.fori_loop(0, step_boxes, one_box, 0)


def translate(own, before, after, far_src, far_class, table, rows, steps):
    block = own.shape[0]
    n_groups = len(before)
    box = lax.axis_index("box")
    half = lax.axis_size("box") // 2
    first_box = (box - 1) * block
    index = jnp.where(far_src >= 0, jnp.clip(far_src - first_box, 0, 3 * block - 1), 3 * block)
    flags = jnp.stack([box == half, box == half - 1]).astype(jnp.int32)
    any_spec = pl.BlockSpec(memory_space=pl.ANY)
    halos = [a for group in before for a in group] + [a for group in after for a in group]
    step_boxes = block // steps
    body = lambda *refs: translate_kernel(block, n_groups, (rows, own.shape[3]), step_boxes, *refs)
    return pl.pallas_call(
        body,
        out_shape=jax.ShapeDtypeStruct(own.shape, jnp.float32),
        grid_spec=pltpu.PrefetchScalarGridSpec(
            num_scalar_prefetch=3,
            grid=(steps,),
            in_specs=[any_spec] * (2 + len(halos)),
            out_specs=pl.BlockSpec(
                (step_boxes,) + own.shape[1:], lambda i, *_: (i, 0, 0, 0)
            ),
            scratch_shapes=[
                pltpu.VMEM((3 * block + 1,) + own.shape[1:], jnp.float32),
                pltpu.VMEM(table.shape, jnp.float32),
                pltpu.SemaphoreType.DMA((2 + 2 * n_groups,)),
            ],
        ),
        name="translate_%d" % block,
    )(flags, index.reshape(-1), far_class.reshape(-1), own, table, *halos)


def on_device(
    low_field,
    far_src_low,
    far_class_low,
    table_low,
    far_src_mid,
    far_class_mid,
    table_mid,
    far_src_top,
    far_class_top,
    table_top,
):
    low_block = low_field.shape[0]
    flip = lax.axis_size("dir") // 2
    low_boxes = to_boxes(low_field)
    parts = 2
    size = low_block // parts
    halos = [halo(low_field[g * size : (g + 1) * size], flip) for g in range(parts)]
    low_before, low_after = zip(*halos)
    mid_boxes = aggregate(low_boxes)
    mid_field = to_polar(mid_boxes)
    mid_before, mid_after = halo(mid_field, 0)
    top_boxes = aggregate(mid_boxes)
    top_field = to_polar(top_boxes)
    top_before, top_after = halo(top_field, 0)
    incoming_low = translate(
        low_field, low_before, low_after, far_src_low, far_class_low, table_low, 16, 8
    )
    incoming_mid = translate(
        mid_field, (mid_before,), (mid_after,), far_src_mid, far_class_mid, table_mid, 8, 4
    )
    incoming_top = translate(
        top_field, (top_before,), (top_after,), far_src_top, far_class_top, table_top, 8, 4
    )
    return (incoming_low, incoming_mid, incoming_top)


def solution(mesh):
    pattern = P("box", None, "dir", None)
    lists = P("box", None)
    table = P(None, None, "dir", None)
    return jax.shard_map(
        on_device,
        mesh=mesh,
        in_specs=(pattern, lists, lists, table, lists, lists, table, lists, lists, table),
        out_specs=(pattern, pattern, pattern),
        check_vma=False,
    )
```

```python
import jax
import jax.numpy as jnp
import numpy as np
from jax import lax
from jax.experimental import pallas as pl
from jax.experimental.pallas import tpu as pltpu
from jax.sharding import PartitionSpec as P

SLOTS = 8
PIECES = 4
ROW = 4


def interp_matrix(samples):
    k = np.arange(2 * samples)[:, None] - 2 * np.arange(samples)[None, :]
    sign = np.where(k % 2 == 0, 0.0, np.where(k % 4 == 1, 1.0, -1.0))
    half = np.pi * np.where(k == 0, 1, k) / (2.0 * samples)
    return np.where(k == 0, 1.0, sign * np.cos(half) / (samples * np.sin(half)))


def split_matrix(matrix):
    high = matrix.astype(np.float32).astype(jnp.bfloat16)
    low = (matrix - high.astype(np.float64)).astype(np.float32).astype(jnp.bfloat16)
    return high, low


def shift_factors(own_rows, azimuth_count):
    dirs, part = lax.axis_size("dir"), lax.axis_index("dir")
    polar_count = 2 * dirs * own_rows
    even = 2 * (part * own_rows + jnp.arange(own_rows, dtype=jnp.int32))
    odd = 2 * jnp.arange(dirs * own_rows, dtype=jnp.int32) + 1
    polar_rows = jnp.concatenate([even, odd])
    polar = jnp.pi * (polar_rows.astype(jnp.float32) + 0.5) / polar_count
    azimuth = (
        2.0
        * jnp.pi
        * jnp.arange(azimuth_count, dtype=jnp.int32).astype(jnp.float32)
        / azimuth_count
    )
    octant = jnp.arange(4, dtype=jnp.int32)
    sign_x = (octant % 2 * 2 - 1).astype(jnp.float32)[:, None, None]
    sign_y = (octant // 2 % 2 * 2 - 1).astype(jnp.float32)[:, None, None]
    wavenumber = polar_count / 8.0
    sin_polar = jnp.sin(polar)[None, :, None]
    cos_polar = jnp.cos(polar)[None, :, None]
    phases = wavenumber * (
        sign_x * sin_polar * jnp.cos(azimuth)[None, None, :]
        + sign_y * sin_polar * jnp.sin(azimuth)[None, None, :]
        - cos_polar
    )
    return (jnp.cos(phases), jnp.sin(phases))


def split_value(x):
    high = x.astype(jnp.bfloat16)
    return high, (x - high.astype(jnp.float32)).astype(jnp.bfloat16)


def aggregate_kernel(x_ref, azimuth_ref, polar_ref, cos_ref, sin_ref, even_ref, odd_ref, refined):
    parents, _, own_rows, _ = even_ref.shape
    parts = odd_ref.shape[0]
    dot = lambda a, b: jnp.dot(a, b, preferred_element_type=jnp.float32)
    for g in range(parents):
        both = []
        for p in range(4):
            first = [x_ref[8 * g + p, part] for part in range(2)]
            second = [x_ref[8 * g + 7 - p, part] for part in range(2)]
            both += [a + b for a, b in zip(first, second)] + [a - b for a, b in zip(first, second)]
        high, low = split_value(jnp.concatenate(both, axis=0))
        wide = dot(jnp.concatenate([high, low, high], axis=1), azimuth_ref[...])
        high, low = split_value(wide)
        for n in range(16):
            r = slice(n * own_rows, (n + 1) * own_rows)
            refined[n, :own_rows] = wide[r]
            columns = jnp.concatenate([high[r], low[r], high[r]], axis=0)
            refined[n, own_rows:] = dot(polar_ref[...], columns)
        for part in range(parts + 1):

            def tile(t, carry, g=g, part=part):
                r = pl.ds(pl.multiple_of(part * own_rows + t * 8, 8), 8)
                real = imag = None
                for p in range(4):
                    c, s = cos_ref[p, r, :], sin_ref[p, r, :]
                    re = c * refined[4 * p, r, :] - s * refined[4 * p + 3, r, :]
                    im = c * refined[4 * p + 1, r, :] + s * refined[4 * p + 2, r, :]
                    real = re if real is None else real + re
                    imag = im if imag is None else imag + im
                o = pl.ds(pl.multiple_of(t * 8, 8), 8)
                if part == 0:
                    even_ref[g, 0, o, :] = real
                    even_ref[g, 1, o, :] = imag
                else:
                    odd_ref[part - 1, g, 0, o, :] = real
                    odd_ref[part - 1, g, 1, o, :] = imag
                return carry

            lax.fori_loop(0, own_rows // 8, tile, 0, unroll=True)


def aggregate(children, factors, group):
    boxes, _, own_rows, azimuth_count = children.shape
    dirs = lax.axis_size("dir")
    rows, columns, parents = dirs * own_rows, 256, boxes // 8
    high, low = split_matrix(interp_matrix(azimuth_count).T)
    azimuth_matrix = np.concatenate([high, high, low], axis=0)
    high, low = (m.reshape(rows, dirs, own_rows) for m in split_matrix(interp_matrix(rows)[1::2]))
    polar_matrices = jnp.asarray(np.concatenate([high, high, low], axis=2).swapaxes(0, 1))
    polar_matrix = lax.dynamic_index_in_dim(
        polar_matrices, lax.axis_index("dir"), 0, keepdims=False
    )
    table_spec = pl.BlockSpec((4, own_rows + rows, columns), lambda i, j: (0, 0, j))
    return pl.pallas_call(
        aggregate_kernel,
        out_shape=(
            jax.ShapeDtypeStruct((parents, 2, own_rows, 2 * azimuth_count), jnp.float32),
            jax.ShapeDtypeStruct((dirs, parents, 2, own_rows, 2 * azimuth_count), jnp.float32),
        ),
        grid=(parents // group, 2 * azimuth_count // columns),
        in_specs=[
            pl.BlockSpec((8 * group, 2, own_rows, azimuth_count), lambda i, j: (i, 0, 0, 0)),
            pl.BlockSpec((3 * azimuth_count, columns), lambda i, j: (0, j)),
            pl.BlockSpec(polar_matrix.shape, lambda i, j: (0, 0)),
            table_spec,
            table_spec,
        ],
        out_specs=(
            pl.BlockSpec((group, 2, own_rows, columns), lambda i, j: (i, 0, 0, j)),
            pl.BlockSpec((dirs, group, 2, own_rows, columns), lambda i, j: (0, i, 0, 0, j)),
        ),
        scratch_shapes=[pltpu.VMEM((16, own_rows + rows, columns), jnp.float32)],
    )(children, jnp.asarray(azimuth_matrix), polar_matrix, *factors)


def join_kernel(even_ref, odd_ref, out_ref, woven):
    boxes, _, rows, columns = even_ref.shape
    n = 0
    for b in range(boxes):
        for part in range(2):
            for c in range(0, columns, 128):
                lanes = pl.ds(c, 128)
                odd = odd_ref[0, b, part, :, lanes]
                for d in range(1, odd_ref.shape[0]):
                    odd = odd + odd_ref[d, b, part, :, lanes]
                woven[n, pl.ds(0, rows, stride=2), :] = even_ref[b, part, :, lanes]
                woven[n, pl.ds(1, rows, stride=2), :] = odd
                out_ref[b, part, :, lanes] = woven[n]
                n += 1


def join(even, odd, group):
    boxes, _, rows, columns = even.shape
    return pl.pallas_call(
        join_kernel,
        out_shape=jax.ShapeDtypeStruct((boxes, 2, 2 * rows, columns), jnp.float32),
        grid=(boxes // group,),
        in_specs=[
            pl.BlockSpec((group, 2, rows, columns), lambda i: (i, 0, 0, 0)),
            pl.BlockSpec((odd.shape[0], group, 2, rows, columns), lambda i: (0, i, 0, 0, 0)),
        ],
        out_specs=pl.BlockSpec((group, 2, 2 * rows, columns), lambda i: (i, 0, 0, 0)),
        scratch_shapes=[pltpu.VMEM((group * columns // 64, 2 * rows, 128), jnp.float32)],
    )(even, odd)


def exchange(partial_sums):
    return lax.all_to_all(partial_sums, "dir", split_axis=0, concat_axis=0, tiled=True)


def over_dirs(pairs, flip):
    dirs = lax.axis_size("dir")
    return [(i * dirs + d, j * dirs + (d ^ flip)) for i, j in pairs for d in range(dirs)]


def send(pattern, pairs, flip=0):
    return lax.ppermute(pattern, ("box", "dir"), over_dirs(pairs, flip))


def halo(pattern, with_middle):
    boxes = lax.axis_size("box")
    half = boxes // 2
    up = [(i, i + 1) for i in range(boxes - 1) if with_middle or i + 1 != half]
    return send(pattern, up), send(pattern, [(j, i) for i, j in up])


def translate_kernel(block, pieces, rows, step_boxes, *refs):
    flags_ref, code_ref, own_ref, table_ref, before_ref, after_ref = refs[:6]
    piece_refs = refs[6 : 6 + pieces]
    out_ref, extended, table, sem = refs[6 + pieces :]
    step = pl.program_id(0)

    @pl.when(step == 0)
    def _():
        sides = (extended.at[pl.ds(0, block)], extended.at[pl.ds(2 * block, block)])
        copies = [
            pltpu.make_async_copy(own_ref, extended.at[pl.ds(block, block)], sem.at[0]),
            pltpu.make_async_copy(table_ref, table, sem.at[1]),
        ]
        for copy in copies:
            copy.start()
        for n, (ref, side) in enumerate(zip((before_ref, after_ref), sides)):
            whole = pltpu.make_async_copy(ref, side, sem.at[2 + n])
            copies.append(whole)
            if not pieces:
                whole.start()
                continue

            @pl.when(flags_ref[n] == 0)
            def _(whole=whole):
                whole.start()

            @pl.when(flags_ref[n] != 0)
            def _(side=side, n=n):
                size = block // pieces
                for g, piece in enumerate(piece_refs):
                    part = side.at[pl.ds(g * size, size)]
                    pltpu.make_async_copy(piece, part, sem.at[2 + n]).start()

        extended[3 * block] = jnp.zeros(extended.shape[1:], jnp.float32)
        for copy in copies:
            copy.wait()

    all_rows = extended.shape[2]

    def one_box(b, carry):
        first = (step * step_boxes + b) * SLOTS
        codes = [code_ref[first + m] for m in range(SLOTS)]
        indices = [c >> 8 for c in codes]
        classes = [c & 255 for c in codes]

        def one_chunk(c, carry):
            r = pl.ds(pl.multiple_of(c * rows, 8), rows)
            real = imag = None
            for i, k in zip(indices, classes):
                p_re, p_im = extended[i, 0, r, :], extended[i, 1, r, :]
                q_re, q_im = table[k, 0, r, :], table[k, 1, r, :]
                re = q_re * p_re - q_im * p_im
                im = q_re * p_im + q_im * p_re
                real = re if real is None else real + re
                imag = im if imag is None else imag + im
            out_ref[b, 0, r, :] = real
            out_ref[b, 1, r, :] = imag
            return carry

        if all_rows == rows:
            return one_chunk(0, carry)
        return lax.fori_loop(0, all_rows // rows, one_chunk, carry)

    lax.fori_loop(0, step_boxes, one_box, 0)


def list_codes(block, far_src, far_class):
    first_box = (lax.axis_index("box") - 1) * block
    index = jnp.where(far_src >= 0, jnp.clip(far_src - first_box, 0, 3 * block - 1), 3 * block)
    return (index * 256 + far_class).reshape(-1)


def translate(own, before, after, pieces, codes, flags, table, rows, steps):
    block = own.shape[0]
    any_spec = pl.BlockSpec(memory_space=pl.ANY)
    step_boxes = block // steps
    body = lambda *refs: translate_kernel(block, len(pieces), rows, step_boxes, *refs)
    return pl.pallas_call(
        body,
        out_shape=jax.ShapeDtypeStruct(own.shape, jnp.float32),
        grid_spec=pltpu.PrefetchScalarGridSpec(
            num_scalar_prefetch=2,
            grid=(steps,),
            in_specs=[any_spec] * (4 + len(pieces)),
            out_specs=pl.BlockSpec(
                (step_boxes,) + own.shape[1:], lambda i, *_: (i, 0, 0, 0)
            ),
            scratch_shapes=[
                pltpu.VMEM((3 * block + 1,) + own.shape[1:], jnp.float32),
                pltpu.VMEM(table.shape, jnp.float32),
                pltpu.SemaphoreType.DMA((4,)),
            ],
        ),
    )(flags, codes, own, table, before, after, *pieces)


def on_device(
    low_field,
    far_src_low,
    far_class_low,
    table_low,
    far_src_mid,
    far_class_mid,
    table_mid,
    far_src_top,
    far_class_top,
    table_top,
):
    low_block = low_field.shape[0]
    flip = lax.axis_size("dir") // 2
    boxes = lax.axis_size("box")
    middle = [(boxes // 2 - 1, boxes // 2), (boxes // 2, boxes // 2 - 1)]
    low_before, low_after = halo(low_field, False)
    size = low_block // PIECES
    cut = [low_field[g * size : (g + 1) * size] for g in range(PIECES)]
    stops = [boxes - ROW, ROW - 1]
    outward = [(i, r) for (i, _), r in zip(middle, stops)]
    inward = [(r, j) for (_, j), r in zip(middle, stops)]
    far = send(send(cut[0], outward), inward)
    crossed = [send(cut[g + 1], middle, flip) for g in range(2)]
    fixed = [send(piece, [(i, i) for i, _ in middle], flip) for piece in crossed]
    low_pieces = [far] + fixed + [send(cut[3], middle)]

    box, half = lax.axis_index("box"), boxes // 2
    flags = jnp.stack([box == half, box == half - 1]).astype(jnp.int32)
    codes = (
        list_codes(low_block, far_src_low, far_class_low),
        list_codes(low_block // 8, far_src_mid, far_class_mid),
        list_codes(low_block // 64, far_src_top, far_class_top),
    )
    own_rows, azimuth = low_field.shape[2:]
    mid_factors = shift_factors(own_rows, 2 * azimuth)
    top_factors = shift_factors(2 * own_rows, 4 * azimuth)

    even, odd = aggregate(low_field, mid_factors, 2)
    odd = exchange(odd)
    odd, flags, codes, top_factors = lax.optimization_barrier((odd, flags, codes, top_factors))
    mid_field = join(even, odd, 8)
    mid_before, mid_after = halo(mid_field, False)
    size = mid_field.shape[0] // 2
    far = send(mid_field[:size], outward)
    mid_pieces = [send(far, inward), send(mid_field[size:], middle)]
    even, odd = aggregate(mid_field, top_factors, 1)
    odd = exchange(odd)
    top_field = join(even, odd, 1)
    top_before, top_after = halo(top_field, True)
    incoming_low = translate(
        *(low_field, low_before, low_after, low_pieces, codes[0], flags, table_low, 16, 8),
    )
    incoming_mid = translate(
        *(mid_field, mid_before, mid_after, mid_pieces, codes[1], flags, table_mid, 8, 4),
    )
    codes_top, incoming_mid = lax.optimization_barrier((codes[2], incoming_mid))
    incoming_top = translate(
        top_field, top_before, top_after, (), codes_top, flags, table_top, 8, 4
    )
    return (incoming_low, incoming_mid, incoming_top)


def solution(mesh):
    pattern = P("box", None, "dir", None)
    lists = P("box", None)
    table = P(None, None, "dir", None)

    return jax.shard_map(
        on_device,
        mesh=mesh,
        in_specs=(pattern, lists, lists, table, lists, lists, table, lists, lists, table),
        out_specs=(pattern, pattern, pattern),
        check_vma=False,
    )
```

```python
import jax
import jax.numpy as jnp
import numpy as np
from jax import lax
from jax.experimental import pallas as pl
from jax.experimental.pallas import tpu as pltpu
from jax.sharding import PartitionSpec as P

SLOTS = 8
ROW = 4


def interp_matrix(samples):
    k = np.arange(2 * samples)[:, None] - 2 * np.arange(samples)[None, :]
    sign = np.where(k % 2 == 0, 0.0, np.where(k % 4 == 1, 1.0, -1.0))
    half = np.pi * np.where(k == 0, 1, k) / (2.0 * samples)
    return np.where(k == 0, 1.0, sign * np.cos(half) / (samples * np.sin(half)))


def split_matrix(matrix):
    high = matrix.astype(np.float32).astype(jnp.bfloat16)
    low = (matrix - high.astype(np.float64)).astype(np.float32).astype(jnp.bfloat16)
    return high, low


def shift_factors(polar_rows, polar_count, azimuth_count, lib):
    polar = lib.pi * (polar_rows + 0.5) / polar_count
    azimuth = 2.0 * lib.pi * lib.arange(azimuth_count) / azimuth_count
    octant = lib.arange(4)
    sign_x = (octant % 2 * 2 - 1)[:, None, None]
    sign_y = (octant // 2 % 2 * 2 - 1)[:, None, None]
    wavenumber = polar_count / 8.0
    sin_polar = lib.sin(polar)[None, :, None]
    cos_polar = lib.cos(polar)[None, :, None]
    phases = wavenumber * (
        sign_x * sin_polar * lib.cos(azimuth)[None, None, :]
        + sign_y * sin_polar * lib.sin(azimuth)[None, None, :]
        - cos_polar
    )
    return lib.cos(phases), lib.sin(phases)


def constant_factors(own_rows, azimuth_count):
    count = 2 * lax.axis_size("dir") * own_rows
    tables = [
        table
        for first in range(2)
        for table in shift_factors(np.arange(first, count, 2), count, azimuth_count, np)
    ]
    return [jnp.asarray(table.astype(np.float32)) for table in tables]


def traced_factors(own_rows, azimuth_count):
    dirs = lax.axis_size("dir")
    count = 2 * dirs * own_rows
    even = 2 * (lax.axis_index("dir") * own_rows + jnp.arange(own_rows, dtype=jnp.int32))
    odd = 2 * jnp.arange(dirs * own_rows, dtype=jnp.int32) + 1
    rows = jnp.concatenate([even, odd]).astype(jnp.float32)
    tables = shift_factors(rows, count, azimuth_count, jnp)
    return [t[:, :own_rows] for t in tables] + [t[:, own_rows:] for t in tables]


def split_value(x):
    high = x.astype(jnp.bfloat16)
    return high, (x - high.astype(jnp.float32)).astype(jnp.bfloat16)


def aggregate_kernel(_, x_ref, azimuth_ref, polar_ref, *refs):
    tables, (even_ref, odd_ref, refined) = (refs[:2], refs[2:4]), refs[4:]
    parents, _, own_rows, _ = even_ref.shape
    parts = odd_ref.shape[0]
    dot = lambda a, b: jnp.dot(a, b, preferred_element_type=jnp.float32)
    for g in range(parents):
        both = []
        for p in range(4):
            first = [x_ref[8 * g + p, part] for part in range(2)]
            second = [x_ref[8 * g + 7 - p, part] for part in range(2)]
            both += [a + b for a, b in zip(first, second)] + [a - b for a, b in zip(first, second)]
        high, low = split_value(jnp.concatenate(both, axis=0))
        wide = dot(jnp.concatenate([high, low, high], axis=1), azimuth_ref[...])
        high, low = split_value(wide)
        for n in range(16):
            r = slice(n * own_rows, (n + 1) * own_rows)
            refined[n, :own_rows] = wide[r]
            columns = jnp.concatenate([high[r], low[r], high[r]], axis=0)
            refined[n, own_rows:] = dot(polar_ref[...], columns)
        for part in range(parts + 1):

            def tile(t, carry, g=g, part=part):
                r = pl.ds(pl.multiple_of(part * own_rows + t * 8, 8), 8)
                at = pl.ds(pl.multiple_of(max(part - 1, 0) * own_rows + t * 8, 8), 8)
                real = imag = None
                for p in range(4):
                    c, s = (table[p, at, :] for table in tables[min(part, 1)])
                    re = c * refined[4 * p, r, :] - s * refined[4 * p + 3, r, :]
                    im = c * refined[4 * p + 1, r, :] + s * refined[4 * p + 2, r, :]
                    real = re if real is None else real + re
                    imag = im if imag is None else imag + im
                o = pl.ds(pl.multiple_of(t * 8, 8), 8)
                if part == 0:
                    even_ref[g, 0, o, :] = real
                    even_ref[g, 1, o, :] = imag
                else:
                    odd_ref[part - 1, g, 0, o, :] = real
                    odd_ref[part - 1, g, 1, o, :] = imag
                return carry

            lax.fori_loop(0, own_rows // 8, tile, 0, unroll=True)


def aggregate(children, factors, group):
    boxes, _, own_rows, azimuth_count = children.shape
    dirs = lax.axis_size("dir")
    rows, columns, parents = dirs * own_rows, 256, boxes // 8
    high, low = split_matrix(interp_matrix(azimuth_count).T)
    azimuth_matrix = np.concatenate([high, high, low], axis=0)
    high, low = (m.reshape(rows, dirs, own_rows) for m in split_matrix(interp_matrix(rows)[1::2]))
    polar_matrices = jnp.asarray(np.concatenate([high, high, low], axis=2).swapaxes(0, 1))
    whole = factors[0].shape[1] > own_rows
    even_spec = pl.BlockSpec(
        (4, own_rows, columns), lambda i, j, d: (0, d[0] if whole else 0, j)
    )
    odd_spec = pl.BlockSpec((4, rows, columns), lambda i, j, d: (0, 0, j))
    return pl.pallas_call(
        aggregate_kernel,
        out_shape=(
            jax.ShapeDtypeStruct((parents, 2, own_rows, 2 * azimuth_count), jnp.float32),
            jax.ShapeDtypeStruct((dirs, parents, 2, own_rows, 2 * azimuth_count), jnp.float32),
        ),
        grid_spec=pltpu.PrefetchScalarGridSpec(
            num_scalar_prefetch=1,
            grid=(parents // group, 2 * azimuth_count // columns),
            in_specs=[
                pl.BlockSpec((8 * group, 2, own_rows, azimuth_count), lambda i, j, d: (i, 0, 0, 0)),
                pl.BlockSpec((3 * azimuth_count, columns), lambda i, j, d: (0, j)),
                pl.BlockSpec((None, rows, 3 * own_rows), lambda i, j, d: (d[0], 0, 0)),
                even_spec,
                even_spec,
                odd_spec,
                odd_spec,
            ],
            out_specs=(
                pl.BlockSpec((group, 2, own_rows, columns), lambda i, j, d: (i, 0, 0, j)),
                pl.BlockSpec((dirs, group, 2, own_rows, columns), lambda i, j, d: (0, i, 0, 0, j)),
            ),
            scratch_shapes=[pltpu.VMEM((16, own_rows + rows, columns), jnp.float32)],
        ),
    )(
        lax.axis_index("dir").astype(jnp.int32).reshape(1),
        children,
        jnp.asarray(azimuth_matrix),
        polar_matrices,
        *factors,
    )


def join_kernel(even_ref, odd_ref, out_ref, woven):
    boxes, _, rows, columns = even_ref.shape
    n = 0
    for b in range(boxes):
        for part in range(2):
            for c in range(0, columns, 128):
                lanes = pl.ds(c, 128)
                odd = odd_ref[0, b, part, :, lanes]
                for d in range(1, odd_ref.shape[0]):
                    odd = odd + odd_ref[d, b, part, :, lanes]
                woven[n, pl.ds(0, rows, stride=2), :] = even_ref[b, part, :, lanes]
                woven[n, pl.ds(1, rows, stride=2), :] = odd
                out_ref[b, part, :, lanes] = woven[n]
                n += 1


def join(even, odd, group):
    boxes, _, rows, columns = even.shape
    return pl.pallas_call(
        join_kernel,
        out_shape=jax.ShapeDtypeStruct((boxes, 2, 2 * rows, columns), jnp.float32),
        grid=(boxes // group,),
        in_specs=[
            pl.BlockSpec((group, 2, rows, columns), lambda i: (i, 0, 0, 0)),
            pl.BlockSpec((odd.shape[0], group, 2, rows, columns), lambda i: (0, i, 0, 0, 0)),
        ],
        out_specs=pl.BlockSpec((group, 2, 2 * rows, columns), lambda i: (i, 0, 0, 0)),
        scratch_shapes=[pltpu.VMEM((group * columns // 64, 2 * rows, 128), jnp.float32)],
    )(even, odd)


def exchange(partial_sums):
    return lax.all_to_all(partial_sums, "dir", split_axis=0, concat_axis=0, tiled=True)


def over_dirs(pairs, flip):
    dirs = lax.axis_size("dir")
    return [(i * dirs + d, j * dirs + (d ^ flip)) for i, j in pairs for d in range(dirs)]


def send(pattern, pairs, flip=0):
    return lax.ppermute(pattern, ("box", "dir"), over_dirs(pairs, flip))


def halo(pattern, with_middle):
    boxes = lax.axis_size("box")
    half = boxes // 2
    up = [(i, i + 1) for i in range(boxes - 1) if with_middle or i + 1 != half]
    return send(pattern, up), send(pattern, [(j, i) for i, j in up])


def routes(pairs, stops):
    return [(i, r) for (i, _), r in zip(pairs, stops)], [(r, j) for (_, j), r in zip(pairs, stops)]


def translate_kernel(block, pieces, rows, step_boxes, *refs):
    flags_ref, code_ref, own_ref, table_ref, before_ref, after_ref = refs[:6]
    piece_refs = refs[6 : 6 + pieces]
    out_ref, extended, table, sem = refs[6 + pieces :]
    step = pl.program_id(0)

    @pl.when(step == 0)
    def _():
        sides = (extended.at[pl.ds(0, block)], extended.at[pl.ds(2 * block, block)])
        copies = [
            pltpu.make_async_copy(own_ref, extended.at[pl.ds(block, block)], sem.at[0]),
            pltpu.make_async_copy(table_ref, table, sem.at[1]),
        ]
        for copy in copies:
            copy.start()
        for n, (ref, side) in enumerate(zip((before_ref, after_ref), sides)):
            whole = pltpu.make_async_copy(ref, side, sem.at[2 + n])
            copies.append(whole)
            if not pieces:
                whole.start()
                continue

            @pl.when(flags_ref[n] == 0)
            def _(whole=whole):
                whole.start()

            @pl.when(flags_ref[n] != 0)
            def _(side=side, n=n):
                start = 0
                for piece in piece_refs:
                    part = side.at[pl.ds(start, piece.shape[0])]
                    pltpu.make_async_copy(piece, part, sem.at[2 + n]).start()
                    start += piece.shape[0]

        extended[3 * block] = jnp.zeros(extended.shape[1:], jnp.float32)
        for copy in copies:
            copy.wait()

    all_rows = extended.shape[2]

    def one_box(b, carry):
        first = (step * step_boxes + b) * SLOTS
        codes = [code_ref[first + m] for m in range(SLOTS)]
        filled = [(c >> 8) < 3 * block for c in codes]

        def add(slots):
            def one_chunk(c, carry):
                r = pl.ds(pl.multiple_of(c * rows, 8), rows)
                real = imag = None
                for code in codes[:slots]:
                    i, k = code >> 8, code & 255
                    p_re, p_im = extended[i, 0, r, :], extended[i, 1, r, :]
                    q_re, q_im = table[k, 0, r, :], table[k, 1, r, :]
                    re = q_re * p_re - q_im * p_im
                    im = q_re * p_im + q_im * p_re
                    real = re if real is None else real + re
                    imag = im if imag is None else imag + im
                out_ref[b, 0, r, :] = real
                out_ref[b, 1, r, :] = imag
                return carry

            if all_rows == rows:
                one_chunk(0, 0)
            else:
                lax.fori_loop(0, all_rows // rows, one_chunk, 0)

        if all_rows == rows:
            add(SLOTS)
            return carry
        for slots in range(2, SLOTS + 1, 2):
            here = filled[slots - 2] if slots > 2 else True
            if slots < SLOTS:
                here = jnp.logical_and(here, jnp.logical_not(filled[slots]))
            pl.when(here)(lambda slots=slots: add(slots))
        return carry

    lax.fori_loop(0, step_boxes, one_box, 0)


def list_codes(block, far_src, far_class):
    first_box = (lax.axis_index("box") - 1) * block
    index = jnp.where(far_src >= 0, jnp.clip(far_src - first_box, 0, 3 * block - 1), 3 * block)
    return (index * 256 + far_class).reshape(-1)


def translate(own, before, after, pieces, codes, flags, table, rows, steps):
    block = own.shape[0]
    any_spec = pl.BlockSpec(memory_space=pl.ANY)
    step_boxes = block // steps
    body = lambda *refs: translate_kernel(block, len(pieces), rows, step_boxes, *refs)
    return pl.pallas_call(
        body,
        out_shape=jax.ShapeDtypeStruct(own.shape, jnp.float32),
        grid_spec=pltpu.PrefetchScalarGridSpec(
            num_scalar_prefetch=2,
            grid=(steps,),
            in_specs=[any_spec] * (4 + len(pieces)),
            out_specs=pl.BlockSpec(
                (step_boxes,) + own.shape[1:], lambda i, *_: (i, 0, 0, 0)
            ),
            scratch_shapes=[
                pltpu.VMEM((3 * block + 1,) + own.shape[1:], jnp.float32),
                pltpu.VMEM(table.shape, jnp.float32),
                pltpu.SemaphoreType.DMA((4,)),
            ],
        ),
    )(flags, codes, own, table, before, after, *pieces)


def on_device(
    low_field,
    far_src_low,
    far_class_low,
    table_low,
    far_src_mid,
    far_class_mid,
    table_mid,
    far_src_top,
    far_class_top,
    table_top,
):
    low_block = low_field.shape[0]
    flip = lax.axis_size("dir") // 2
    boxes = lax.axis_size("box")
    middle = [(boxes // 2 - 1, boxes // 2), (boxes // 2, boxes // 2 - 1)]
    low_before, low_after = halo(low_field, False)
    rows = [boxes - ROW, ROW - 1]
    ends = [boxes - 1, 0]
    cut = [low_block * n // 32 for n in (9, 18, 30)]
    to_rows, from_rows = routes(middle, rows)
    to_ends, from_ends = routes(middle, ends)
    by_rows = send(low_field[: cut[0]], to_rows)
    by_rows = send(by_rows, from_rows)
    by_ends = send(low_field[cut[0] : cut[1]], to_ends)
    by_ends = send(by_ends, from_ends)

    box, half = lax.axis_index("box"), boxes // 2
    flags = jnp.stack([box == half, box == half - 1]).astype(jnp.int32)
    codes = (
        list_codes(low_block, far_src_low, far_class_low),
        list_codes(low_block // 8, far_src_mid, far_class_mid),
        list_codes(low_block // 64, far_src_top, far_class_top),
    )
    own_rows, azimuth = low_field.shape[2:]
    mid_factors = constant_factors(own_rows, 2 * azimuth)
    top_factors = traced_factors(2 * own_rows, 4 * azimuth)

    even, odd = aggregate(low_field, mid_factors, 4)
    odd, later_low = lax.optimization_barrier((odd, low_field))
    odd = exchange(odd)
    swap = send(later_low[cut[1] : cut[2]], middle, flip)
    swap = send(swap, [(i, i) for i, _ in middle], flip)
    direct = send(later_low[cut[2] :], middle)
    low_pieces = [by_rows, by_ends, swap, direct]
    odd, flags, codes, top_factors = lax.optimization_barrier((odd, flags, codes, top_factors))
    mid_field = join(even, odd, 16)
    mid_before, mid_after = halo(mid_field, False)
    half_mid = mid_field.shape[0] // 2
    by_ends = send(mid_field[:half_mid], to_ends, flip)
    mid_pieces = [send(by_ends, from_ends, flip), send(mid_field[half_mid:], middle)]
    even, odd = aggregate(mid_field, top_factors, 1)
    odd = exchange(odd)
    top_field = join(even, odd, 1)
    top_before, top_after = halo(top_field, True)
    incoming_low = translate(
        *(low_field, low_before, low_after, low_pieces, codes[0], flags, table_low, 16, 8),
    )
    incoming_mid = translate(
        *(mid_field, mid_before, mid_after, mid_pieces, codes[1], flags, table_mid, 8, 4),
    )
    codes_top, incoming_mid = lax.optimization_barrier((codes[2], incoming_mid))
    incoming_top = translate(
        top_field, top_before, top_after, (), codes_top, flags, table_top, 8, 4
    )
    return (incoming_low, incoming_mid, incoming_top)


def solution(mesh):
    pattern = P("box", None, "dir", None)
    lists = P("box", None)
    table = P(None, None, "dir", None)

    return jax.shard_map(
        on_device,
        mesh=mesh,
        in_specs=(pattern, lists, lists, table, lists, lists, table, lists, lists, table),
        out_specs=(pattern, pattern, pattern),
        check_vma=False,
    )
```
